32 devices in a mesh: slab: 4 (over y, x), box: 8 (over z, core).
Axes of the slice: x: 2, y: 2, z: 4, core: 2. Of those that a mesh axis runs over, the one named last changes fastest.
Arguments:
- sources: bfloat16 [4, 8, 512, 4096], P('slab', 'box'), may hold values from -6 to 6
- leaf_ops: bfloat16 [4, 8, 256, 4096], P('slab', 'box'), may hold values from -0.09375 to 0.09375
- edge_slot: int32 [4, 8, 256], P('slab', 'box'), may hold values from 0 to 255, each once within a row
- merge_ops: float32 [4, 8, 256, 256], P('slab', 'box'), may hold values from -0.25 to 0.25
- lift_ops: float32 [4, 8, 512, 256], P('slab', 'box'), may hold values from -0.375 to 0.375
- coupling: float32 [4, 512, 512], P('slab', 'box'), may hold values from -0.125 to 0.125
- inverse: float32 [4, 512, 512], P('slab', 'box'), may hold values from -0.25 to 0.25
- boundary: float32 [512, 512], P(None, 'box'), may hold values from -6 to 6
Outputs:
- interface_solution: float32 [4, 512, 512], P('slab', None, 'box')
The draws below stay inside these ranges and needn't reach their ends.
Inputs may be any that keep to these rules, and one draw needn't show every extreme that they name: Each row edge_slot[s, b] holds every number from 0 to 255 once.
All inputs are finite; a program needn't handle non-finite values.
Results may differ from the reference program's by a relative error of at most 0.0003.
Values sent between devices are 32-bit elements; how exact they have to be, the bound alone decides.
A program may use at most 64 MiB of HBM per device.

```python
import jax
import jax.numpy as jnp
from jax import lax

E = 256
P_SIZE = 4096
NI = 512
R = 512
SLABS = 4
BOXES = 8
LEVELS = 3


def level_of(key, shape, shards, smallest, top_value):
    factor_of, own = 1.0, jax.random.fold_in(key, 6)
    for dim, parts in shards:
        steps = jnp.exp(jax.random.uniform(jax.random.fold_in(own, dim), (parts,), jnp.float32, smallest / len(shards), top_value / len(shards)))
        factor_of = factor_of * jnp.repeat(steps, shape[dim] // parts).reshape([-1 if axis == dim else 1 for axis in range(len(shape))])
    return factor_of


def centred(own_key, dims, width, reach, shards=(), held_as=jnp.bfloat16):
    factor_of = level_of(own_key, dims, shards, -0.22, 0.18) if shards else 1.0
    result = jax.random.normal(own_key, dims, jnp.float32) * width * factor_of
    return jnp.minimum(jnp.maximum(result, -reach), reach).astype(held_as)


def setup_inputs(seed: int = 0) -> dict:
    key_list = jax.random.split(jax.random.key(seed), 9)
    return {
        "sources": centred(key_list[0], (SLABS, BOXES, R, P_SIZE), 1.0, 6.0, ((0, 4), (1, 8))),
        "leaf_ops": centred(key_list[1], (SLABS, BOXES, E, P_SIZE), P_SIZE ** -0.5, 0.09375, ((0, 4), (1, 8))),
        "edge_slot": jax.vmap(lambda own: jax.random.permutation(own, E))(jax.random.split(key_list[2], SLABS * BOXES)).reshape((SLABS, BOXES, E)).astype(jnp.int32),
        "merge_ops": centred(key_list[3], (SLABS, BOXES, E, E), (2 * E) ** -0.5, 0.25, ((0, 4), (1, 8)), jnp.float32),
        "lift_ops": centred(key_list[4], (SLABS, BOXES, NI, E), E ** -0.5, 0.375, ((0, 4), (1, 8)), jnp.float32),
        "coupling": centred(key_list[5], (SLABS, NI, NI), (4 * NI) ** -0.5, 0.125, ((0, 4), (1, 8)), jnp.float32),
        "inverse": centred(key_list[6], (SLABS, NI, NI), NI ** -0.5, 0.25, ((0, 4), (1, 8)), jnp.float32),
        "boundary": centred(key_list[7], (R, NI), 1.0, 6.0, ((1, 8),), jnp.float32),
    }


highest = lax.Precision.HIGHEST


def reorder(box_flux, slot_row):
    return jnp.take(box_flux, slot_row, axis=1)


def reference(sources, leaf_ops, edge_slot, merge_ops, lift_ops, coupling, inverse, boundary):
    previous = boundary
    outputs = []
    box_ids = jnp.arange(BOXES, dtype=jnp.int32)
    for slab_index in range(SLABS):
        box_flux = jnp.einsum("brp,bep->bre", sources[slab_index].astype(jnp.float32), leaf_ops[slab_index].astype(jnp.float32), precision=highest)
        current = jax.vmap(reorder)(box_flux, edge_slot[slab_index])
        for tree_level in range(LEVELS):
            bit_number = LEVELS - 1 - tree_level
            merged = jnp.einsum("bre,bfe->brf", current, merge_ops[slab_index], precision=highest)
            partner = jnp.bitwise_xor(box_ids, jnp.int32(2 ** bit_number))
            summed = merged + merged[partner]
            half_rows = summed.shape[1] // 2
            upper_half = jnp.bitwise_and(jnp.right_shift(box_ids, bit_number), 1)
            current = jnp.where((upper_half == 1)[:, None, None], summed[:, half_rows:], summed[:, :half_rows])
        lifted = jnp.einsum("bre,bie->bri", current, lift_ops[slab_index], precision=highest)
        slab_load = lifted.reshape(R, NI)
        corrected = slab_load - jnp.dot(previous, coupling[slab_index].T, precision=highest, preferred_element_type=jnp.float32)
        previous = jnp.dot(corrected, inverse[slab_index].T, precision=highest, preferred_element_type=jnp.float32)
        outputs.append(previous)
    return jnp.stack(outputs)
```

```python
import jax
import jax.numpy as jnp
from jax import lax
from jax.sharding import PartitionSpec as P

high = lax.Precision.HIGH
contract_last = (((1,), (1,)), ((), ()))


def mm_t(a, b, dims=contract_last):
    return lax.dot_general(a, b, dims, precision=high, preferred_element_type=jnp.float32)


def on_device(sources, leaf_ops, edge_slot, merge_ops, lift_ops, coupling, inverse, boundary):
    slot_box = edge_slot[0, 0]
    merge_box = merge_ops[0, 0]
    lift_box = lift_ops[0, 0]
    coupling_all = lax.all_gather(coupling[0], "box", axis=0, tiled=True)
    inverse_all = lax.all_gather(inverse[0], "box", axis=0, tiled=True)
    edges = slot_box.shape[0]
    onehot = (slot_box[:, None] == lax.broadcasted_iota(jnp.int32, (edges, edges), 1)).astype(jnp.float32)
    first = mm_t(merge_box, onehot, (((1,), (0,)), ((), ())))
    entering = lax.all_to_all(boundary, "box", split_axis=0, concat_axis=1, tiled=True)
    current = lax.dot_general(
        sources[0, 0], leaf_ops[0, 0], contract_last, preferred_element_type=jnp.float32
    )
    n_box = lax.axis_size("box")
    levels = n_box.bit_length() - 1
    position = lax.axis_index("box")
    for level in range(levels):
        bit = levels - 1 - level
        merged = mm_t(current, first if level == 0 else merge_box)
        half = current.shape[0] // 2
        upper = jnp.bitwise_and(jnp.right_shift(position, bit), 1)
        kept = lax.dynamic_slice_in_dim(merged, upper * half, half, 0)
        given = lax.dynamic_slice_in_dim(merged, (1 - upper) * half, half, 0)
        pairs = [(i, i ^ (1 << bit)) for i in range(n_box)]
        current = kept + lax.ppermute(given, "box", pairs)
    load = mm_t(current, lift_box)
    own = mm_t(load, inverse_all)
    carry = mm_t(inverse_all, coupling_all, (((1,), (0,)), ((), ())))
    n_slab = lax.axis_size("slab")
    slab = lax.axis_index("slab")
    incoming = entering
    for section in range(n_slab):
        state = own - mm_t(incoming, carry)
        if section + 1 < n_slab:
            passed = lax.ppermute(state, "slab", [(i, i + 1) for i in range(n_slab - 1)])
            incoming = jnp.where(slab == 0, entering, passed)
    return lax.all_to_all(state, "box", split_axis=1, concat_axis=0, tiled=True)[None]


def solution(mesh):
    return jax.shard_map(
        on_device,
        mesh=mesh,
        in_specs=(
            P("slab", "box", None, None),
            P("slab", "box", None, None),
            P("slab", "box", None),
            P("slab", "box", None, None),
            P("slab", "box", None, None),
            P("slab", "box", None),
            P("slab", "box", None),
            P(None, "box"),
        ),
        out_specs=P("slab", None, "box"),
        check_vma=False,
    )
```

```python
import functools

import jax
import jax.numpy as jnp
from jax import lax
from jax.experimental import pallas as pl
from jax.experimental.pallas import tpu as pltpu
from jax.sharding import PartitionSpec as P

MESH = pl.DeviceIdType.MESH
contract_last = (((1,), (1,)), ((), ()))
DEPTH_CHUNKS = 4
CHAIN_CHUNKS = 1


def dot_t(a, b):
    return lax.dot_general(a, b, contract_last, preferred_element_type=jnp.float32)


def halves(x):
    hi = x.astype(jnp.bfloat16)
    return hi, (x - hi.astype(jnp.float32)).astype(jnp.bfloat16)


def dot3(x, w_hi, w_lo):
    hi, lo = halves(x)
    return dot_t(hi, w_hi) + (dot_t(hi, w_lo) + dot_t(lo, w_hi))


def kernel(
    n, n_slab, split_ahead,
    src, leaf, slot, merge, lift, coup, inv, bnd, out,
    sv, lv, mv, ltv, full, split, lift_split, xb, kept, lsend, lrecv,
    bb, pv, st, ob,
    loc, lev_s, lev_r, g_s, g_r, p_s, p_r, ch_s, ch_r, o_s, o_r, b_s, b_r,
):
    me, slab = lax.axis_index("box"), lax.axis_index("slab")
    chips = n // 2
    chip = me // 2
    core = me - 2 * chip
    mate = me + 1 - 2 * core
    rows, points = pv.shape
    width = points // n
    total, edges = lsend.shape
    half0 = total // 2
    depth = lv.shape[1]
    kd = depth // DEPTH_CHUNKS
    levels = n.bit_length() - 1
    shards = (coup, inv)

    def side(level):
        mask = 2 ** (levels - 1 - level)
        bit = lax.rem(me // mask, 2)
        return bit, me + mask - 2 * mask * bit

    bit0, _ = side(0)
    starts = ((1 - bit0) * half0, bit0 * half0)

    local = []

    def read(a, b):
        c = pltpu.make_async_copy(a, b, loc.at[len(local)])
        c.start()
        local.append(c)
        return c

    read_merge = read(merge, mv)
    read_leaf, read_src = [], ([], [])
    for which in range(2):
        for k in range(DEPTH_CHUNKS):
            cols = pl.ds(k * kd, kd)
            if which == 0:
                read_leaf.append(read(leaf.at[:, cols], lv.at[:, cols]))
            at = pl.ds(pl.multiple_of(starts[which], half0), half0)
            read_src[which].append(read(src.at[at, cols], sv.at[which, :, cols]))
    read_lift = read(lift, ltv)

    def shard_at(i, owner):
        return full.at[i, pl.ds(pl.multiple_of(owner * width, width), width), :]

    read_own = [read(shards[i], shard_at(i, me)) for i in range(2)]

    barrier = pltpu.get_barrier_semaphore()
    for d in range(1, n):
        pl.semaphore_signal(
            barrier, inc=1, device_id={"box": lax.rem(me + d, n)}, device_id_type=MESH
        )
    for d in (1, n_slab - 1):
        pl.semaphore_signal(
            barrier, inc=1, device_id={"slab": lax.rem(slab + d, n_slab)}, device_id_type=MESH
        )
    pl.semaphore_wait(barrier, n + 1)

    def remote(a, b, s, r, to, axis="box"):
        return pltpu.make_async_remote_copy(
            src_ref=a, dst_ref=b, send_sem=s, recv_sem=r,
            device_id={axis: to}, device_id_type=MESH,
        )

    def line(direction, t, i):
        step = 1 if direction == 0 else -1
        owner = me - 2 * step * t
        ok_chip = chip - step * t
        to_chip = chip + step
        a = shards[i] if t == 0 else shard_at(i, owner)
        ok = (ok_chip >= 0) & (ok_chip < chips) & (to_chip >= 0) & (to_chip < chips)
        return ok, remote(
            a, shard_at(i, owner), g_s.at[direction, t, i], g_r.at[direction, t, i], me + 2 * step
        )

    def arrival(direction, t, i):
        step = 1 if direction == 0 else -1
        ref = shard_at(i, me - 2 * step * (t + 1))
        return remote(
            ref, ref, g_s.at[direction, t, i], g_r.at[direction, t, i], me - 2 * step
        )

    def came(direction, t):
        owner_chip = chip - (t + 1 if direction == 0 else -t - 1)
        return (owner_chip >= 0) & (owner_chip < chips)

    def share(direction, t, i):
        step = 1 if direction == 0 else -1
        owner = me - 2 * step * (t + 1)
        k = 0 if t < 0 else 1 + 2 * t + direction
        a = shards[i] if t < 0 else shard_at(i, owner)
        return remote(a, shard_at(i, owner), p_s.at[k, i], p_r.at[k, i], mate)

    def shared(direction, t, i):
        step = 1 if direction == 0 else -1
        k = 0 if t < 0 else 1 + 2 * t + direction
        ref = shard_at(i, mate - 2 * step * (t + 1))
        return remote(ref, ref, p_s.at[k, i], p_r.at[k, i], mate)

    def launch(t):
        for direction in range(2):
            for i in range(2):
                ok, copy = line(direction, t, i)
                pl.when(ok)(copy.start)

    def take(t):
        for direction in range(2):
            for i in range(2):
                pl.when(came(direction, t))(arrival(direction, t, i).wait_recv)
        if t + 1 < chips - 1:
            launch(t + 1)
        for direction in range(2):
            for i in range(2):
                pl.when(came(direction, t))(share(direction, t, i).start)

    launch(0)
    for i in range(2):
        share(0, -1, i).start()

    def rows_of(who):
        return pl.ds(pl.multiple_of(who * rows, rows), rows)

    @pl.when(slab == 0)
    def _():
        pltpu.make_async_copy(bnd.at[rows_of(me), :], bb.at[me], b_s.at[0]).start()
        for d in range(1, n):
            to = lax.rem(me + d, n)
            remote(bnd.at[rows_of(to), :], bb.at[me], b_s.at[d], b_r.at[d], to).start()

    read_merge.wait()
    m_hi, m_lo = halves(mv[...])
    place = (
        lax.broadcasted_iota(jnp.int32, (edges, edges), 0) == slot[...]
    ).astype(jnp.float32).astype(jnp.bfloat16)
    first = (dot_t(m_hi, place).astype(jnp.bfloat16), dot_t(m_lo, place).astype(jnp.bfloat16))

    def flux(which):
        acc = None
        for k in range(DEPTH_CHUNKS):
            if which == 0:
                read_leaf[k].wait()
            read_src[which][k].wait()
            cols = slice(k * kd, (k + 1) * kd)
            part = dot_t(sv[which, :, cols], lv[:, cols])
            acc = part if acc is None else acc + part
        return acc

    offset = 0
    sent = []
    for level in range(levels):
        bit, to = side(level)
        half = total >> (level + 1)
        area = pl.ds(offset, half)
        offset += half

        def part_of(which):
            if level == 0:
                return dot3(flux(which), *first)
            at = bit if which == 1 else 1 - bit
            x = xb[pl.ds(pl.multiple_of(at * half, half), half), :]
            return dot3(x, m_hi, m_lo)

        lsend[area, :] = part_of(0)
        copy = remote(lsend.at[area, :], lrecv.at[area, :], lev_s.at[level], lev_r.at[level], to)
        copy.start()
        sent.append(copy)
        kept[pl.ds(0, half), :] = part_of(1)
        if level == 0:
            read_lift.wait()
            lift_split[0], lift_split[1] = halves(ltv[...])
            for c in read_own:
                c.wait()
        if level < chips - 1:
            take(level)
        copy.wait_recv()
        xb[pl.ds(0, half), :] = kept[pl.ds(0, half), :] + lrecv[area, :]

    load = dot3(xb[pl.ds(0, rows), :], lift_split[0], lift_split[1])

    for t in range(levels, chips - 1):
        take(t)
    for i in range(2):
        shared(0, -1, i).wait_recv()
    for t in range(chips - 1):
        for direction in range(2):
            for i in range(2):
                pl.when(came(direction, t))(shared(direction, t, i).wait_recv)

    block = min(points, 256)
    if split_ahead:
        for i in range(2):
            for r in range(0, points, block):
                hi, lo = halves(full[i, r : r + block, :])
                split[2 * i, r : r + block, :] = hi
                split[2 * i + 1, r : r + block, :] = lo

    def times(x, i):
        if split_ahead:
            return dot3(x, split[2 * i], split[2 * i + 1])
        parts = [dot3(x, *halves(full[i, r : r + block, :])) for r in range(0, points, block)]
        return jnp.concatenate(parts, axis=1)

    @pl.when(slab == 0)
    def _():
        pltpu.make_async_copy(bnd.at[rows_of(me), :], bb.at[me], b_s.at[0]).wait()
        for d in range(1, n):
            who = lax.rem(me + n - d, n)
            remote(bb.at[who], bb.at[who], b_s.at[d], b_r.at[d], who).wait_recv()
        for j in range(n):
            pv[:, j * width : (j + 1) * width] = bb[j]

    def hop(c):
        at = pl.ds(c * (rows // CHAIN_CHUNKS), rows // CHAIN_CHUNKS)
        return remote(
            st.at[at, :], pv.at[at, :], ch_s.at[c], ch_r.at[c],
            lax.rem(slab + 1, n_slab), "slab",
        )

    for c in range(CHAIN_CHUNKS):
        lo_row = c * (rows // CHAIN_CHUNKS)
        hi_row = lo_row + rows // CHAIN_CHUNKS
        pl.when(slab > 0)(hop(c).wait_recv)
        corrected = load[lo_row:hi_row] - times(pv[lo_row:hi_row, :], 0)
        state = times(corrected, 1)
        st[lo_row:hi_row, :] = state
        pl.when(slab < n_slab - 1)(hop(c).start)
        for j in range(n):
            ob[j, lo_row:hi_row, :] = state[:, j * width : (j + 1) * width]

    own = pltpu.make_async_copy(ob.at[me], out.at[rows_of(me), :], o_s.at[0])
    own.start()
    outs = []
    for d in range(1, n):
        to = lax.rem(me + d, n)
        copy = remote(ob.at[to], out.at[rows_of(me), :], o_s.at[d], o_r.at[d], to)
        copy.start()
        outs.append(copy)

    for copy in sent:
        copy.wait_send()
    for i in range(2):
        share(0, -1, i).wait_send()
    for t in range(chips - 1):
        for direction in range(2):
            for i in range(2):
                ok, copy = line(direction, t, i)
                pl.when(ok)(copy.wait_send)
                pl.when(came(direction, t))(share(direction, t, i).wait_send)

    @pl.when(slab == 0)
    def _():
        for d in range(1, n):
            to = lax.rem(me + d, n)
            remote(bnd.at[rows_of(to), :], bb.at[me], b_s.at[d], b_r.at[d], to).wait_send()

    for c in range(CHAIN_CHUNKS):
        pl.when(slab < n_slab - 1)(hop(c).wait_send)
    own.wait()
    for d in range(1, n):
        outs[d - 1].wait_send()
        who = lax.rem(me + n - d, n)
        remote(ob.at[who], out.at[rows_of(who), :], o_s.at[d], o_r.at[d], who).wait_recv()


def on_device(sources, leaf_ops, edge_slot, merge_ops, lift_ops, coupling, inverse, boundary):
    n, n_slab = lax.axis_size("box"), lax.axis_size("slab")
    total, depth = sources.shape[2:]
    edges = leaf_ops.shape[2]
    points = lift_ops.shape[2]
    rows, width = total // n, points // n
    chips, levels = n // 2, n.bit_length() - 1
    split_ahead = points * points <= 2**20
    f32, bf16 = jnp.float32, jnp.bfloat16
    hbm = pl.BlockSpec(memory_space=pl.ANY)
    dma = lambda *s: pltpu.SemaphoreType.DMA(s)
    result = pl.pallas_call(
        functools.partial(kernel, n, n_slab, split_ahead),
        out_shape=jax.ShapeDtypeStruct((total, width), f32),
        in_specs=[hbm, hbm, pl.BlockSpec(memory_space=pltpu.VMEM)] + [hbm] * 5,
        out_specs=hbm,
        scratch_shapes=[
            pltpu.VMEM((2, total // 2, depth), bf16),
            pltpu.VMEM((edges, depth), bf16),
            pltpu.VMEM((edges, edges), f32),
            pltpu.VMEM((points, edges), f32),
            pltpu.VMEM((2, points, points), f32),
            pltpu.VMEM((4, points, points) if split_ahead else (4, 16, 128), bf16),
            pltpu.VMEM((2, points, edges), bf16),
            pltpu.VMEM((total // 2, edges), f32),
            pltpu.VMEM((total // 2, edges), f32),
            pltpu.VMEM((total, edges), f32),
            pltpu.VMEM((total, edges), f32),
            pltpu.VMEM((n, rows, width), f32),
            pltpu.VMEM((rows, points), f32),
            pltpu.VMEM((rows, points), f32),
            pltpu.VMEM((n, rows, width), f32),
            dma(3 * DEPTH_CHUNKS + 4),
            dma(levels), dma(levels),
            dma(2, chips - 1, 2), dma(2, chips - 1, 2),
            dma(2 * chips, 2), dma(2 * chips, 2),
            dma(CHAIN_CHUNKS), dma(CHAIN_CHUNKS),
            dma(n), dma(n), dma(n), dma(n),
        ],
        compiler_params=pltpu.CompilerParams(collective_id=0, has_side_effects=True),
        name="slab_solve",
    )(
        sources[0, 0], leaf_ops[0, 0], edge_slot[0], merge_ops[0, 0], lift_ops[0, 0],
        coupling[0], inverse[0], boundary,
    )
    return result[None]


def solution(mesh):
    return jax.shard_map(
        on_device,
        mesh=mesh,
        in_specs=(
            P("slab", "box", None, None),
            P("slab", "box", None, None),
            P("slab", "box", None),
            P("slab", "box", None, None),
            P("slab", "box", None, None),
            P("slab", "box", None),
            P("slab", "box", None),
            P(None, "box"),
        ),
        out_specs=P("slab", None, "box"),
        check_vma=False,
    )
```

```python
import functools

import jax
import jax.numpy as jnp
from jax import lax
from jax.experimental import pallas as pl
from jax.experimental.pallas import tpu as pltpu
from jax.sharding import PartitionSpec as P

MESH = pl.DeviceIdType.MESH
contract_last = (((1,), (1,)), ((), ()))
DEPTH_CHUNKS = 2
CHAIN_CHUNKS = 2


def dot_t(a, b):
    return lax.dot_general(a, b, contract_last, preferred_element_type=jnp.float32)


def halves(x):
    hi = x.astype(jnp.bfloat16)
    return hi, (x - hi.astype(jnp.float32)).astype(jnp.bfloat16)


def dot3(x, w_hi, w_lo):
    hi, lo = halves(x)
    return dot_t(hi, w_hi) + (dot_t(hi, w_lo) + dot_t(lo, w_hi))


def kernel(
    n, n_slab, split_ahead,
    src, leaf, slot, merge, lift, coup, inv, bnd, out,
    sv, lv, mv, ltv, full, split, lift_split, lsend, lrecv,
    bst, bv, pv, st, cz, ob, rb,
    loc, lev_s, lev_r, g_s, g_r, p_s, p_r, ch_s, ch_r, o_s, o_r, b_s, b_r, x_s, x_r,
):
    me, slab = lax.axis_index("box"), lax.axis_index("slab")
    chips = n // 2
    chip = me // 2
    core = me - 2 * chip
    mate = me + 1 - 2 * core
    rows, points = pv.shape
    width = points // n
    total, edges = lsend.shape
    depth = lv.shape[1]
    kd = depth // DEPTH_CHUNKS
    levels = n.bit_length() - 1
    aid = split_ahead
    helper = n_slab - 1 if aid else 0
    is_helper = slab == helper
    coup0 = 2 if aid else 0

    def peer(level):
        mask = 2 ** (levels - 1 - level)
        return me + mask - 2 * mask * lax.rem(me // mask, 2)

    def block_of(position):
        block = 0
        for q in range(levels):
            bit = lax.rem(me // 2**q, 2)
            block = block + 2**q * (bit if (position >> q) & 1 else 1 - bit)
        return block

    local = []

    def read(a, b):
        c = pltpu.make_async_copy(a, b, loc.at[len(local)])
        c.start()
        local.append(c)
        return c

    def rows_of(who):
        return pl.ds(pl.multiple_of(who * rows, rows), rows)

    read_merge = read(merge, mv)
    read_leaf, read_src = [], ([], [])
    for which in range(2):
        for k in range(DEPTH_CHUNKS):
            cols = pl.ds(k * kd, kd)
            if which == 0:
                read_leaf.append(read(leaf.at[:, cols], lv.at[:, cols]))
            read_src[which].append([
                read(src.at[rows_of(block_of(p)), cols], sv.at[pl.ds(p * rows, rows), cols])
                for p in range(which * n // 2, (which + 1) * n // 2)
            ])
    read_lift = read(lift, ltv)

    def shard_at(i, owner):
        return full.at[i, pl.ds(pl.multiple_of(owner * width, width), width), :]

    read_own = [read(m, shard_at(i, me)) for i, m in enumerate((coup, inv))]

    barrier = pltpu.get_barrier_semaphore()
    for d in range(1, n):
        pl.semaphore_signal(
            barrier, inc=1, device_id={"box": lax.rem(me + d, n)}, device_id_type=MESH
        )
    for d in (1, n_slab - 1):
        pl.semaphore_signal(
            barrier, inc=1, device_id={"slab": lax.rem(slab + d, n_slab)}, device_id_type=MESH
        )
    pl.semaphore_wait(barrier, n + 1)

    def remote(a, b, s, r, to, axis="box"):
        return pltpu.make_async_remote_copy(
            src_ref=a, dst_ref=b, send_sem=s, recv_sem=r,
            device_id={axis: to}, device_id_type=MESH,
        )

    def line(direction, t, i):
        step = 1 if direction == 0 else -1
        owner = me - 2 * step * t
        ok_chip = chip - step * t
        to_chip = chip + step
        a = (coup, inv)[i] if t == 0 and i < 2 else shard_at(i, owner)
        ok = (ok_chip >= 0) & (ok_chip < chips) & (to_chip >= 0) & (to_chip < chips)
        return ok, remote(
            a, shard_at(i, owner), g_s.at[direction, t, i], g_r.at[direction, t, i], me + 2 * step
        )

    def arrival(direction, t, i):
        step = 1 if direction == 0 else -1
        ref = shard_at(i, me - 2 * step * (t + 1))
        return remote(
            ref, ref, g_s.at[direction, t, i], g_r.at[direction, t, i], me - 2 * step
        )

    def came(direction, t):
        owner_chip = chip - (t + 1 if direction == 0 else -t - 1)
        return (owner_chip >= 0) & (owner_chip < chips)

    def share(direction, t, i):
        step = 1 if direction == 0 else -1
        owner = me - 2 * step * (t + 1)
        k = 0 if t < 0 else 1 + 2 * t + direction
        a = (coup, inv)[i] if t < 0 and i < 2 else shard_at(i, owner)
        return remote(a, shard_at(i, owner), p_s.at[k, i], p_r.at[k, i], mate)

    def shared(direction, t, i):
        step = 1 if direction == 0 else -1
        k = 0 if t < 0 else 1 + 2 * t + direction
        ref = shard_at(i, mate - 2 * step * (t + 1))
        return remote(ref, ref, p_s.at[k, i], p_r.at[k, i], mate)

    def launch(t, i):
        if t == 0:
            share(0, -1, i).start()
        for direction in range(2):
            ok, copy = line(direction, t, i)
            pl.when(ok)(copy.start)

    def take(t, i):
        for direction in range(2):
            pl.when(came(direction, t))(arrival(direction, t, i).wait_recv)
        if t + 1 < chips - 1:
            launch(t + 1, i)
        for direction in range(2):
            pl.when(came(direction, t))(share(direction, t, i).start)

    def all_here(i):
        shared(0, -1, i).wait_recv()
        for t in range(chips - 1):
            for direction in range(2):
                pl.when(came(direction, t))(shared(direction, t, i).wait_recv)

    def all_sent(i):
        share(0, -1, i).wait_send()
        for t in range(chips - 1):
            for direction in range(2):
                ok, copy = line(direction, t, i)
                pl.when(ok)(copy.wait_send)
                pl.when(came(direction, t))(share(direction, t, i).wait_send)

    def coupled(f, *args):
        if aid:
            pl.when(slab != 0)(lambda: f(*args))
        else:
            f(*args)

    def lend():
        return remote(coup, shard_at(2, me), x_s.at[0], x_r.at[0], helper, "slab")

    def answer():
        return remote(st, pv, x_s.at[1], x_r.at[1], 0, "slab")

    def edge_block(d):
        to = lax.rem(me + d, n)
        at = pl.ds(pl.multiple_of(me * width, width), width)
        return remote(bst.at[to], bv.at[at, :], b_s.at[d], b_r.at[d], to)

    own_edge = pltpu.make_async_copy(
        bst.at[me], bv.at[pl.ds(pl.multiple_of(me * width, width), width), :], b_s.at[0]
    )

    if aid:
        pl.when(slab == 0)(lend().start)

    @pl.when(is_helper)
    def _():
        for j in range(n):
            bst[j] = bnd[:, j * rows : (j + 1) * rows]
        own_edge.start()
        for d in range(1, n):
            edge_block(d).start()
        if aid:
            lend().wait_recv()
            launch(0, 2)

    launch(0, 1)
    coupled(launch, 0, 0)

    read_merge.wait()
    m_hi, m_lo = halves(mv[...])
    place = (
        lax.broadcasted_iota(jnp.int32, (edges, edges), 0) == slot[...]
    ).astype(jnp.float32).astype(jnp.bfloat16)
    first = (dot_t(m_hi, place).astype(jnp.bfloat16), dot_t(m_lo, place).astype(jnp.bfloat16))

    def flux(which):
        acc = None
        for k in range(DEPTH_CHUNKS):
            if which == 0:
                read_leaf[k].wait()
            for c in read_src[which][k]:
                c.wait()
            cols = slice(k * kd, (k + 1) * kd)
            part = dot_t(sv[which * total // 2 : (which + 1) * total // 2, cols], lv[:, cols])
            acc = part if acc is None else acc + part
        return acc

    offset = 0
    sent = []
    place_of = []
    for level in range(levels):
        half = total >> (level + 1)
        pieces = 2 if level < levels - 1 else 1
        place_of.append((offset, half // pieces, pieces))
        offset += half

    def give(level, y):
        start, size, pieces = place_of[level]
        lsend[start : start + size * pieces, :] = y
        copies = []
        for c in range(pieces):
            at = pl.ds(start + c * size, size)
            copy = remote(
                lsend.at[at, :], lrecv.at[at, :], lev_s.at[level, c], lev_r.at[level, c], peer(level)
            )
            copy.start()
            copies.append(copy)
        sent.extend(copies)
        return copies

    def got(level, c):
        start, size, _ = place_of[level]
        return lrecv[start + c * size : start + (c + 1) * size, :]

    copies = give(0, dot3(flux(0), *first))
    keep = dot3(flux(1), *first)
    read_lift.wait()
    lift_split[0], lift_split[1] = halves(ltv[...])
    for c in read_own:
        c.wait()

    if aid:
        @pl.when(is_helper)
        def _():
            for t in range(chips - 1):
                take(t, 2)
            all_here(2)
            own_edge.wait()
            for d in range(1, n):
                edge_block(d).wait_recv()
            st[...] = dot3(bv[...].T, *halves(full[2]))
            answer().start()

    taken = 0
    for level in range(levels):
        size = place_of[level][1]
        if taken < chips - 1:
            take(taken, 1)
            coupled(take, taken, 0)
            taken += 1
        copies[0].wait_recv()
        x = keep[:size] + got(level, 0)
        if level < levels - 1:
            later = give(level + 1, dot3(x, m_hi, m_lo))
            copies[1].wait_recv()
            keep = dot3(keep[size:] + got(level, 1), m_hi, m_lo)
            copies = later
    load = dot3(x, lift_split[0], lift_split[1])

    for t in range(taken, chips - 1):
        take(t, 1)
        coupled(take, t, 0)

    block = min(points, 256)

    def prepare(i):
        if split_ahead:
            for r in range(0, points, block):
                hi, lo = halves(full[i, r : r + block, :])
                split[2 * i, r : r + block, :] = hi
                split[2 * i + 1, r : r + block, :] = lo

    all_here(1)
    prepare(1)

    def ready():
        all_here(0)
        prepare(0)

    coupled(ready)

    def rows_at(i, r):
        if split_ahead:
            return split[2 * i, r : r + block, :], split[2 * i + 1, r : r + block, :]
        return halves(full[i, r : r + block, :])

    def times(x, i):
        if split_ahead:
            return dot3(x, split[2 * i], split[2 * i + 1])
        return jnp.concatenate(
            [dot3(x, *rows_at(i, r)) for r in range(0, points, block)], axis=1
        )

    if not aid:
        @pl.when(is_helper)
        def _():
            own_edge.wait()
            for d in range(1, n):
                edge_block(d).wait_recv()
            pv[...] = bv[...].T

    size = rows // CHAIN_CHUNKS

    def hop(c):
        at = pl.ds(c * size, size)
        return remote(
            st.at[at, :], pv.at[at, :], ch_s.at[c], ch_r.at[c],
            lax.rem(slab + 1, n_slab), "slab",
        )

    if aid:
        pl.when(slab == 0)(answer().wait_recv)
    for c in range(CHAIN_CHUNKS):
        at = slice(c * size, (c + 1) * size)
        mine = load[at]

        def later_slab():
            cz[at, :] = mine - times(pv[at, :], 0)

        def first_slab():
            cz[at, :] = mine - pv[at, :]

        pl.when(slab > 0)(hop(c).wait_recv)
        if aid:
            pl.when(slab > 0)(later_slab)
            pl.when(slab == 0)(first_slab)
        else:
            later_slab()

        @pl.when(slab < n_slab - 1)
        def _():
            st[at, :] = times(cz[at, :], 1)
            hop(c).start()

    c_hi, c_lo = halves(cz[...])
    for r in range(0, points, block):
        w_hi, w_lo = rows_at(1, r)
        turned = dot_t(w_hi, c_hi) + (dot_t(w_hi, c_lo) + dot_t(w_lo, c_hi))
        for j in range(block // width):
            ob[r // width + j] = turned[j * width : (j + 1) * width]

    own = pltpu.make_async_copy(ob.at[me], rb.at[me], o_s.at[0])
    own.start()
    outs = []
    for d in range(1, n):
        to = lax.rem(me + d, n)
        copy = remote(ob.at[to], rb.at[me], o_s.at[d], o_r.at[d], to)
        copy.start()
        outs.append(copy)

    for copy in sent:
        copy.wait_send()
    all_sent(1)
    coupled(all_sent, 0)

    @pl.when(is_helper)
    def _():
        for d in range(1, n):
            edge_block(d).wait_send()
        if aid:
            all_sent(2)
            answer().wait_send()

    if aid:
        pl.when(slab == 0)(lend().wait_send)
    for c in range(CHAIN_CHUNKS):
        pl.when(slab < n_slab - 1)(hop(c).wait_send)
    own.wait()
    for d in range(1, n):
        who = lax.rem(me + n - d, n)
        remote(ob.at[who], rb.at[who], o_s.at[d], o_r.at[d], who).wait_recv()
    for j in range(n):
        out[:, j * rows : (j + 1) * rows] = rb[j]
    for copy in outs:
        copy.wait_send()


def on_device(sources, leaf_ops, edge_slot, merge_ops, lift_ops, coupling, inverse, boundary):
    n, n_slab = lax.axis_size("box"), lax.axis_size("slab")
    total, depth = sources.shape[2:]
    edges = leaf_ops.shape[2]
    points = lift_ops.shape[2]
    rows, width = total // n, points // n
    chips, levels = n // 2, n.bit_length() - 1
    split_ahead = points * points <= 2**20
    f32, bf16 = jnp.float32, jnp.bfloat16
    hbm = pl.BlockSpec(memory_space=pl.ANY)
    dma = lambda *s: pltpu.SemaphoreType.DMA(s)
    vmem = pl.BlockSpec(memory_space=pltpu.VMEM)
    result = pl.pallas_call(
        functools.partial(kernel, n, n_slab, split_ahead),
        out_shape=jax.ShapeDtypeStruct((width, total), f32),
        in_specs=[hbm, hbm, vmem] + [hbm] * 4 + [vmem],
        out_specs=vmem,
        scratch_shapes=[
            pltpu.VMEM((total, depth), bf16),
            pltpu.VMEM((edges, depth), bf16),
            pltpu.VMEM((edges, edges), f32),
            pltpu.VMEM((points, edges), f32),
            pltpu.VMEM((3 if split_ahead else 2, points, points), f32),
            pltpu.VMEM((4, points, points) if split_ahead else (4, 16, 128), bf16),
            pltpu.VMEM((2, points, edges), bf16),
            pltpu.VMEM((total, edges), f32),
            pltpu.VMEM((total, edges), f32),
            pltpu.VMEM((n, width, rows), f32),
            pltpu.VMEM((points, rows), f32),
            pltpu.VMEM((rows, points), f32),
            pltpu.VMEM((rows, points), f32),
            pltpu.VMEM((rows, points), f32),
            pltpu.VMEM((n, width, rows), f32),
            pltpu.VMEM((n, width, rows), f32),
            dma(DEPTH_CHUNKS * (n + 1) + 4),
            dma(levels, 2), dma(levels, 2),
            dma(2, chips - 1, 3), dma(2, chips - 1, 3),
            dma(2 * chips, 3), dma(2 * chips, 3),
            dma(CHAIN_CHUNKS), dma(CHAIN_CHUNKS),
            dma(n), dma(n), dma(n), dma(n), dma(2), dma(2),
        ],
        compiler_params=pltpu.CompilerParams(collective_id=0, has_side_effects=True),
        name="slab_solve",
    )(
        sources[0, 0], leaf_ops[0, 0], edge_slot[0], merge_ops[0, 0], lift_ops[0, 0],
        coupling[0], inverse[0], boundary.T,
    )
    return result.T[None]


def solution(mesh):
    return jax.shard_map(
        on_device,
        mesh=mesh,
        in_specs=(
            P("slab", "box", None, None),
            P("slab", "box", None, None),
            P("slab", "box", None),
            P("slab", "box", None, None),
            P("slab", "box", None, None),
            P("slab", "box", None),
            P("slab", "box", None),
            P(None, "box"),
        ),
        out_specs=P("slab", None, "box"),
        check_vma=False,
    )
```

```python
import functools

import jax
import jax.numpy as jnp
from jax import lax
from jax.experimental import pallas as pl
from jax.experimental.pallas import tpu as pltpu
from jax.sharding import PartitionSpec as P

MESH = pl.DeviceIdType.MESH
contract_last = (((1,), (1,)), ((), ()))
DEPTH_CHUNKS = 2
CHAIN_CHUNKS = 4


def dot_t(a, b):
    return lax.dot_general(a, b, contract_last, preferred_element_type=jnp.float32)


def halves(x):
    hi = x.astype(jnp.bfloat16)
    return hi, (x - hi.astype(jnp.float32)).astype(jnp.bfloat16)


def dot3(x, w_hi, w_lo):
    hi, lo = halves(x)
    return dot_t(hi, w_hi) + (dot_t(hi, w_lo) + dot_t(lo, w_hi))


def kernel(
    n, n_slab, split_ahead,
    src, leaf, slot, merge, lift, coup, inv, bnd, out,
    sv, lv, mv, ltv, full, split, lift_split, lsend, lrecv,
    bst, bv, pv, st, cz, ob, rb,
    loc, lev_s, lev_r, g_s, g_r, p_s, p_r, ch_s, ch_r, o_s, o_r, b_s, b_r, x_s, x_r,
):
    me, slab = lax.axis_index("box"), lax.axis_index("slab")
    chips = n // 2
    chip = me // 2
    core = me - 2 * chip
    mate = me + 1 - 2 * core
    rows, points = pv.shape
    width = points // n
    total, edges = lsend.shape
    depth = lv.shape[1]
    kd = depth // DEPTH_CHUNKS
    levels = n.bit_length() - 1
    aid = False
    helper = n_slab - 1 if aid else 0
    is_helper = slab == helper
    coup0 = 2 if aid else 0

    def peer(level):
        mask = 2 ** (levels - 1 - level)
        return me + mask - 2 * mask * lax.rem(me // mask, 2)

    def block_of(position):
        block = 0
        for q in range(levels):
            bit = lax.rem(me // 2**q, 2)
            block = block + 2**q * (bit if (position >> q) & 1 else 1 - bit)
        return block

    local = []

    def read(a, b):
        c = pltpu.make_async_copy(a, b, loc.at[len(local)])
        c.start()
        local.append(c)
        return c

    def rows_of(who):
        return pl.ds(pl.multiple_of(who * rows, rows), rows)

    read_merge = read(merge, mv)
    read_leaf, read_src = [], ([], [])
    for which in range(2):
        for k in range(DEPTH_CHUNKS):
            cols = pl.ds(k * kd, kd)
            if which == 0:
                read_leaf.append(read(leaf.at[:, cols], lv.at[:, cols]))
            read_src[which].append([
                read(src.at[rows_of(block_of(p)), cols], sv.at[pl.ds(p * rows, rows), cols])
                for p in range(which * n // 2, (which + 1) * n // 2)
            ])
    read_lift = read(lift, ltv)

    def shard_at(i, owner):
        return full.at[i, pl.ds(pl.multiple_of(owner * width, width), width), :]

    read_own = [read(m, shard_at(i, me)) for i, m in enumerate((coup, inv))]

    barrier = pltpu.get_barrier_semaphore()
    for d in range(1, n):
        pl.semaphore_signal(
            barrier, inc=1, device_id={"box": lax.rem(me + d, n)}, device_id_type=MESH
        )
    for d in (1, n_slab - 1):
        pl.semaphore_signal(
            barrier, inc=1, device_id={"slab": lax.rem(slab + d, n_slab)}, device_id_type=MESH
        )
    pl.semaphore_wait(barrier, n + 1)

    def remote(a, b, s, r, to, axis="box"):
        return pltpu.make_async_remote_copy(
            src_ref=a, dst_ref=b, send_sem=s, recv_sem=r,
            device_id={axis: to}, device_id_type=MESH,
        )

    def line(direction, t, i):
        step = 1 if direction == 0 else -1
        owner = me - 2 * step * t
        ok_chip = chip - step * t
        to_chip = chip + step
        a = (coup, inv)[i] if t == 0 and i < 2 else shard_at(i, owner)
        ok = (ok_chip >= 0) & (ok_chip < chips) & (to_chip >= 0) & (to_chip < chips)
        return ok, remote(
            a, shard_at(i, owner), g_s.at[direction, t, i], g_r.at[direction, t, i], me + 2 * step
        )

    def arrival(direction, t, i):
        step = 1 if direction == 0 else -1
        ref = shard_at(i, me - 2 * step * (t + 1))
        return remote(
            ref, ref, g_s.at[direction, t, i], g_r.at[direction, t, i], me - 2 * step
        )

    def came(direction, t):
        owner_chip = chip - (t + 1 if direction == 0 else -t - 1)
        return (owner_chip >= 0) & (owner_chip < chips)

    def share(direction, t, i):
        step = 1 if direction == 0 else -1
        owner = me - 2 * step * (t + 1)
        k = 0 if t < 0 else 1 + 2 * t + direction
        a = (coup, inv)[i] if t < 0 and i < 2 else shard_at(i, owner)
        return remote(a, shard_at(i, owner), p_s.at[k, i], p_r.at[k, i], mate)

    def shared(direction, t, i):
        step = 1 if direction == 0 else -1
        k = 0 if t < 0 else 1 + 2 * t + direction
        ref = shard_at(i, mate - 2 * step * (t + 1))
        return remote(ref, ref, p_s.at[k, i], p_r.at[k, i], mate)

    def launch(t, i):
        if t == 0:
            share(0, -1, i).start()
        for direction in range(2):
            ok, copy = line(direction, t, i)
            pl.when(ok)(copy.start)

    def take(t, i):
        for direction in range(2):
            pl.when(came(direction, t))(arrival(direction, t, i).wait_recv)
        if t + 1 < chips - 1:
            launch(t + 1, i)
        for direction in range(2):
            pl.when(came(direction, t))(share(direction, t, i).start)

    def all_here(i):
        shared(0, -1, i).wait_recv()
        for t in range(chips - 1):
            for direction in range(2):
                pl.when(came(direction, t))(shared(direction, t, i).wait_recv)

    def all_sent(i):
        share(0, -1, i).wait_send()
        for t in range(chips - 1):
            for direction in range(2):
                ok, copy = line(direction, t, i)
                pl.when(ok)(copy.wait_send)
                pl.when(came(direction, t))(share(direction, t, i).wait_send)

    def coupled(f, *args):
        if aid:
            pl.when(slab != 0)(lambda: f(*args))
        else:
            f(*args)

    def lend():
        return remote(coup, shard_at(2, me), x_s.at[0], x_r.at[0], helper, "slab")

    def answer():
        return remote(st, pv, x_s.at[1], x_r.at[1], 0, "slab")

    def edge_block(d):
        to = lax.rem(me + d, n)
        at = pl.ds(pl.multiple_of(me * width, width), width)
        return remote(bst.at[to], bv.at[at, :], b_s.at[d], b_r.at[d], to)

    own_edge = pltpu.make_async_copy(
        bst.at[me], bv.at[pl.ds(pl.multiple_of(me * width, width), width), :], b_s.at[0]
    )

    if aid:
        pl.when(slab == 0)(lend().start)

    @pl.when(is_helper)
    def _():
        for j in range(n):
            bst[j] = bnd[:, j * rows : (j + 1) * rows]
        own_edge.start()
        for d in range(1, n):
            edge_block(d).start()
        if aid:
            lend().wait_recv()
            launch(0, 2)

    launch(0, 1)
    coupled(launch, 0, 0)

    read_merge.wait()
    m_hi, m_lo = halves(mv[...])
    place = (
        lax.broadcasted_iota(jnp.int32, (edges, edges), 0) == slot[...]
    ).astype(jnp.float32).astype(jnp.bfloat16)
    first = (dot_t(m_hi, place).astype(jnp.bfloat16), dot_t(m_lo, place).astype(jnp.bfloat16))

    def flux(which):
        acc = None
        for k in range(DEPTH_CHUNKS):
            if which == 0:
                read_leaf[k].wait()
            for c in read_src[which][k]:
                c.wait()
            cols = slice(k * kd, (k + 1) * kd)
            part = dot_t(sv[which * total // 2 : (which + 1) * total // 2, cols], lv[:, cols])
            acc = part if acc is None else acc + part
        return acc

    offset = 0
    sent = []
    place_of = []
    for level in range(levels):
        half = total >> (level + 1)
        pieces = 2 if level < levels - 1 else 1
        place_of.append((offset, half // pieces, pieces))
        offset += half

    def give(level, y):
        start, size, pieces = place_of[level]
        lsend[start : start + size * pieces, :] = y
        copies = []
        for c in range(pieces):
            at = pl.ds(start + c * size, size)
            copy = remote(
                lsend.at[at, :], lrecv.at[at, :], lev_s.at[level, c], lev_r.at[level, c], peer(level)
            )
            copy.start()
            copies.append(copy)
        sent.extend(copies)
        return copies

    def got(level, c):
        start, size, _ = place_of[level]
        return lrecv[start + c * size : start + (c + 1) * size, :]

    copies = give(0, dot3(flux(0), *first))
    keep = dot3(flux(1), *first)
    read_lift.wait()
    lift_split[0], lift_split[1] = halves(ltv[...])
    for c in read_own:
        c.wait()

    if aid:
        @pl.when(is_helper)
        def _():
            for t in range(chips - 1):
                take(t, 2)
            all_here(2)
            own_edge.wait()
            for d in range(1, n):
                edge_block(d).wait_recv()
            st[...] = dot3(bv[...].T, *halves(full[2]))
            answer().start()

    taken = 0
    for level in range(levels):
        size = place_of[level][1]
        if taken < chips - 1:
            take(taken, 1)
            coupled(take, taken, 0)
            taken += 1
        copies[0].wait_recv()
        x = keep[:size] + got(level, 0)
        if level < levels - 1:
            later = give(level + 1, dot3(x, m_hi, m_lo))
            copies[1].wait_recv()
            keep = dot3(keep[size:] + got(level, 1), m_hi, m_lo)
            copies = later
    load = dot3(x, lift_split[0], lift_split[1])

    for t in range(taken, chips - 1):
        take(t, 1)
        coupled(take, t, 0)

    block = min(points, 256)

    def prepare(i):
        if split_ahead:
            for r in range(0, points, block):
                hi, lo = halves(full[i, r : r + block, :])
                split[2 * i, r : r + block, :] = hi
                split[2 * i + 1, r : r + block, :] = lo

    all_here(1)
    prepare(1)

    def ready():
        all_here(0)
        prepare(0)

    coupled(ready)

    def rows_at(i, r):
        if split_ahead:
            return split[2 * i, r : r + block, :], split[2 * i + 1, r : r + block, :]
        return halves(full[i, r : r + block, :])

    def times(x, i):
        if split_ahead:
            return dot3(x, split[2 * i], split[2 * i + 1])
        return jnp.concatenate(
            [dot3(x, *rows_at(i, r)) for r in range(0, points, block)], axis=1
        )

    if not aid:
        @pl.when(is_helper)
        def _():
            own_edge.wait()
            for d in range(1, n):
                edge_block(d).wait_recv()
            pv[...] = bv[...].T

    chunks = max(1, min(CHAIN_CHUNKS, rows // 16))
    size = rows // chunks

    def hop(c):
        at = pl.ds(c * size, size)
        return remote(
            st.at[at, :], pv.at[at, :], ch_s.at[c], ch_r.at[c],
            lax.rem(slab + 1, n_slab), "slab",
        )

    if aid:
        pl.when(slab == 0)(answer().wait_recv)
    for c in range(chunks):
        at = slice(c * size, (c + 1) * size)
        mine = load[at]

        def later_slab():
            cz[at, :] = mine - times(pv[at, :], 0)

        def first_slab():
            cz[at, :] = mine - pv[at, :]

        pl.when(slab > 0)(hop(c).wait_recv)
        if aid:
            pl.when(slab > 0)(later_slab)
            pl.when(slab == 0)(first_slab)
        else:
            later_slab()

        @pl.when(slab < n_slab - 1)
        def _():
            st[at, :] = times(cz[at, :], 1)
            hop(c).start()

    c_hi, c_lo = halves(cz[...])
    for r in range(0, points, block):
        w_hi, w_lo = rows_at(1, r)
        turned = dot_t(w_hi, c_hi) + (dot_t(w_hi, c_lo) + dot_t(w_lo, c_hi))
        for j in range(block // width):
            ob[r // width + j] = turned[j * width : (j + 1) * width]

    own = pltpu.make_async_copy(ob.at[me], rb.at[me], o_s.at[0])
    own.start()
    outs = []
    for d in range(1, n):
        to = lax.rem(me + d, n)
        copy = remote(ob.at[to], rb.at[me], o_s.at[d], o_r.at[d], to)
        copy.start()
        outs.append(copy)

    for copy in sent:
        copy.wait_send()
    all_sent(1)
    coupled(all_sent, 0)

    @pl.when(is_helper)
    def _():
        for d in range(1, n):
            edge_block(d).wait_send()
        if aid:
            all_sent(2)
            answer().wait_send()

    if aid:
        pl.when(slab == 0)(lend().wait_send)
    for c in range(chunks):
        pl.when(slab < n_slab - 1)(hop(c).wait_send)
    own.wait()
    for d in range(1, n):
        who = lax.rem(me + n - d, n)
        remote(ob.at[who], rb.at[who], o_s.at[d], o_r.at[d], who).wait_recv()
    for j in range(n):
        out[:, j * rows : (j + 1) * rows] = rb[j]
    for copy in outs:
        copy.wait_send()


def on_device(sources, leaf_ops, edge_slot, merge_ops, lift_ops, coupling, inverse, boundary):
    n, n_slab = lax.axis_size("box"), lax.axis_size("slab")
    total, depth = sources.shape[2:]
    edges = leaf_ops.shape[2]
    points = lift_ops.shape[2]
    rows, width = total // n, points // n
    chips, levels = n // 2, n.bit_length() - 1
    split_ahead = points * points <= 2**20
    f32, bf16 = jnp.float32, jnp.bfloat16
    hbm = pl.BlockSpec(memory_space=pl.ANY)
    dma = lambda *s: pltpu.SemaphoreType.DMA(s)
    vmem = pl.BlockSpec(memory_space=pltpu.VMEM)
    result = pl.pallas_call(
        functools.partial(kernel, n, n_slab, split_ahead),
        out_shape=jax.ShapeDtypeStruct((width, total), f32),
        in_specs=[hbm, hbm, vmem] + [hbm] * 4 + [vmem],
        out_specs=vmem,
        scratch_shapes=[
            pltpu.VMEM((total, depth), bf16),
            pltpu.VMEM((edges, depth), bf16),
            pltpu.VMEM((edges, edges), f32),
            pltpu.VMEM((points, edges), f32),
            pltpu.VMEM((2, points, points), f32),
            pltpu.VMEM((4, points, points) if split_ahead else (4, 16, 128), bf16),
            pltpu.VMEM((2, points, edges), bf16),
            pltpu.VMEM((total, edges), f32),
            pltpu.VMEM((total, edges), f32),
            pltpu.VMEM((n, width, rows), f32),
            pltpu.VMEM((points, rows), f32),
            pltpu.VMEM((rows, points), f32),
            pltpu.VMEM((rows, points), f32),
            pltpu.VMEM((rows, points), f32),
            pltpu.VMEM((n, width, rows), f32),
            pltpu.VMEM((n, width, rows), f32),
            dma(DEPTH_CHUNKS * (n + 1) + 4),
            dma(levels, 2), dma(levels, 2),
            dma(2, chips - 1, 3), dma(2, chips - 1, 3),
            dma(2 * chips, 3), dma(2 * chips, 3),
            dma(CHAIN_CHUNKS), dma(CHAIN_CHUNKS),
            dma(n), dma(n), dma(n), dma(n), dma(2), dma(2),
        ],
        compiler_params=pltpu.CompilerParams(collective_id=0, has_side_effects=True),
        name="slab_solve",
    )(
        sources[0, 0], leaf_ops[0, 0], edge_slot[0], merge_ops[0, 0], lift_ops[0, 0],
        coupling[0], inverse[0], boundary.T,
    )
    return result.T[None]


def solution(mesh):
    return jax.shard_map(
        on_device,
        mesh=mesh,
        in_specs=(
            P("slab", "box", None, None),
            P("slab", "box", None, None),
            P("slab", "box", None),
            P("slab", "box", None, None),
            P("slab", "box", None, None),
            P("slab", "box", None),
            P("slab", "box", None),
            P(None, "box"),
        ),
        out_specs=P("slab", None, "box"),
        check_vma=False,
    )
```
